32 devices in a mesh: dp: 16 (over z, x, core), tensor: 2 (over y).
Axes of the slice: x: 2, y: 2, z: 4, core: 2. Of those that a mesh axis runs over, the one named last changes fastest.
Arguments:
- entering_activations: float32 [16384, 1024], P(('dp', 'tensor')), may hold values from -6 to 6
- segment_ids: int32 [16, 1024], P('dp'), may hold values from 0 to 7, never falling along the last dimension, each value on 1 to 512 neighbouring positions
- leaving_activation_slope: float32 [16384, 1024], P(('dp', 'tensor')), may hold values from -6 to 6
- qkv_weight: float32 [1024, 3072], P('dp', 'tensor'), may hold values from -0.1875 to 0.1875
- qv_bias: float32 [2048], P('tensor'), may hold values from -1.75 to 1.75
- dense_weight: float32 [1024, 1024], P('tensor', 'dp'), may hold values from -0.5 to 0.5
- dense_bias: float32 [1024], replicated, may hold values from -1.75 to 1.75
- up_weight: float32 [1024, 4096], P('dp', 'tensor'), may hold values from -0.1875 to 0.1875
- up_bias: float32 [4096], P('tensor'), may hold values from -3 to 3
- down_weight: float32 [4096, 1024], P('tensor', 'dp'), may hold values from -0.09375 to 0.09375
- down_bias: float32 [1024], replicated, may hold values from -1.75 to 1.75
- mixer_scale_factor: float32 [1024], replicated, may hold values from 0.1 to 1.9
- mixer_offset_term: float32 [1024], replicated, may hold values from -1.75 to 1.75
- perceptron_scale_factor: float32 [1024], replicated, may hold values from 0.1 to 1.9
- perceptron_offset_term: float32 [1024], replicated, may hold values from -1.75 to 1.75
- first_qkv_weight: float32 [1024, 3072], P('dp', 'tensor'), may hold values from -24 to 24
- first_qv_bias: float32 [2048], P('tensor'), may hold values from -24 to 24
- first_dense_weight: float32 [1024, 1024], P('tensor', 'dp'), may hold values from -24 to 24
- first_dense_bias: float32 [1024], replicated, may hold values from -64 to 64
- first_up_weight: float32 [1024, 4096], P('dp', 'tensor'), may hold values from -24 to 24
- first_up_bias: float32 [4096], P('tensor'), may hold values from -24 to 24
- first_down_weight: float32 [4096, 1024], P('tensor', 'dp'), may hold values from -24 to 24
- first_down_bias: float32 [1024], replicated, may hold values from -64 to 64
- first_norm1_gain: float32 [1024], replicated, may hold values from -64 to 64
- first_norm1_bias: float32 [1024], replicated, may hold values from -64 to 64
- first_norm2_gain: float32 [1024], replicated, may hold values from -64 to 64
- first_norm2_bias: float32 [1024], replicated, may hold values from -64 to 64
- second_qkv_weight: float32 [1024, 3072], P('dp', 'tensor'), may hold values from 64 to 2048
- second_qv_bias: float32 [2048], P('tensor'), may hold values from 64 to 2048
- second_dense_weight: float32 [1024, 1024], P('tensor', 'dp'), may hold values from 64 to 2048
- second_dense_bias: float32 [1024], replicated, may hold values from 1024 to 16384
- second_up_weight: float32 [1024, 4096], P('dp', 'tensor'), may hold values from 64 to 2048
- second_up_bias: float32 [4096], P('tensor'), may hold values from 64 to 2048
- second_down_weight: float32 [4096, 1024], P('tensor', 'dp'), may hold values from 64 to 2048
- second_down_bias: float32 [1024], replicated, may hold values from 1024 to 16384
- second_norm1_gain: float32 [1024], replicated, may hold values from 1024 to 16384
- second_norm1_bias: float32 [1024], replicated, may hold values from 1024 to 16384
- second_norm2_gain: float32 [1024], replicated, may hold values from 1024 to 16384
- second_norm2_bias: float32 [1024], replicated, may hold values from 1024 to 16384
Outputs:
- block_out: float32 [16384, 1024], P(('dp', 'tensor'))
- entering_activation_slope: float32 [16384, 1024], P(('dp', 'tensor'))
- grad_qkv_weight: float32 [1024, 3072], P('dp', 'tensor')
- grad_qv_bias: float32 [2048], P('tensor')
- grad_dense_weight: float32 [1024, 1024], P('tensor', 'dp')
- grad_dense_bias: float32 [1024], replicated
- grad_up_weight: float32 [1024, 4096], P('dp', 'tensor')
- grad_up_bias: float32 [4096], P('tensor')
- grad_down_weight: float32 [4096, 1024], P('tensor', 'dp')
- grad_down_bias: float32 [1024], replicated
- grad_norm1_gain: float32 [1024], replicated
- grad_norm1_bias: float32 [1024], replicated
- grad_norm2_gain: float32 [1024], replicated
- grad_norm2_bias: float32 [1024], replicated
- new_qkv_weight: float32 [1024, 3072], P('dp', 'tensor')
- new_qv_bias: float32 [2048], P('tensor')
- new_dense_weight: float32 [1024, 1024], P('tensor', 'dp')
- new_dense_bias: float32 [1024], replicated
- new_up_weight: float32 [1024, 4096], P('dp', 'tensor')
- new_up_bias: float32 [4096], P('tensor')
- new_down_weight: float32 [4096, 1024], P('tensor', 'dp')
- new_down_bias: float32 [1024], replicated
- new_norm1_gain: float32 [1024], replicated
- new_norm1_bias: float32 [1024], replicated
- new_norm2_gain: float32 [1024], replicated
- new_norm2_bias: float32 [1024], replicated
- new_first_qkv_weight: float32 [1024, 3072], P('dp', 'tensor')
- new_first_qv_bias: float32 [2048], P('tensor')
- new_first_dense_weight: float32 [1024, 1024], P('tensor', 'dp')
- new_first_dense_bias: float32 [1024], replicated
- new_first_up_weight: float32 [1024, 4096], P('dp', 'tensor')
- new_first_up_bias: float32 [4096], P('tensor')
- new_first_down_weight: float32 [4096, 1024], P('tensor', 'dp')
- new_first_down_bias: float32 [1024], replicated
- new_first_norm1_gain: float32 [1024], replicated
- new_first_norm1_bias: float32 [1024], replicated
- new_first_norm2_gain: float32 [1024], replicated
- new_first_norm2_bias: float32 [1024], replicated
- new_second_qkv_weight: float32 [1024, 3072], P('dp', 'tensor')
- new_second_qv_bias: float32 [2048], P('tensor')
- new_second_dense_weight: float32 [1024, 1024], P('tensor', 'dp')
- new_second_dense_bias: float32 [1024], replicated
- new_second_up_weight: float32 [1024, 4096], P('dp', 'tensor')
- new_second_up_bias: float32 [4096], P('tensor')
- new_second_down_weight: float32 [4096, 1024], P('tensor', 'dp')
- new_second_down_bias: float32 [1024], replicated
- new_second_norm1_gain: float32 [1024], replicated
- new_second_norm1_bias: float32 [1024], replicated
- new_second_norm2_gain: float32 [1024], replicated
- new_second_norm2_bias: float32 [1024], replicated
The draws below stay inside these ranges and needn't reach their ends.
Inputs may be any that keep to these rules, and one draw needn't show every extreme that they name: Along each row of segment_ids the numbers never fall.
All inputs are finite; a program needn't handle non-finite values.
Results may differ from the reference program's by a relative error of at most 0.019.
Values may be sent and summed in bfloat16 or wider, within the bound.
A program may use at most 256 MiB of HBM per device.

```python
import math
import jax
import jax.numpy as jnp
import numpy as np
from jax import lax

D = 1024
FOCUS_COUNT = 16
FF = 4096
SEQ_LEN = 1024
DOCS = 8
ADAM_STEP = 4
HEAD_DIM = 64
SEQS = 16
TOKENS = 16384
N_TENSOR = 2


def level_of(rng, extent, shards, smallest, top_value):
    gain, own = 1.0, jax.random.fold_in(rng, 6)
    for dim, blocks in shards:
        steps = jnp.exp(jax.random.uniform(jax.random.fold_in(own, dim), (blocks,), jnp.float32, smallest / len(shards), top_value / len(shards)))
        gain = gain * jnp.repeat(steps, extent[dim] // blocks).reshape([-1 if axis == dim else 1 for axis in range(len(extent))])
    return gain


def length_profile(number_of, total, bound, skew):
    portions = [(1 << 20) // math.isqrt(rank ** skew) + 1 for rank in range(2, number_of + 1)]
    rest, holding = total - bound - (number_of - 1), [1] * (number_of - 1)
    while rest > 0:
        free = [i for i in range(number_of - 1) if holding[i] < bound]
        whole, left = sum([portions[i] for i in free]), rest
        for i in free:
            more = min(bound - holding[i], max(1, left * portions[i] // whole), rest)
            holding[i] = holding[i] + more
            rest = rest - more
    return np.array([bound] + holding)


def ragged(rng, amount, total, bound, lean):
    if amount == 2:
        one = jax.random.randint(rng, (), max(1, total - bound), min(bound, total - 1) + 1)
        return jnp.stack([one, total - one])
    sizes = jnp.asarray(length_profile(amount, total, bound, lean), jnp.int32)
    couples = (amount - 1) // 2
    source_of, receiver = sizes[1:1 + 2 * couples:2], sizes[2:2 + 2 * couples:2]
    slack = jnp.minimum(source_of - 1, bound - receiver)
    shifted = jax.random.randint(jax.random.fold_in(rng, 1), (couples,), 0, 1 << 20) % (slack + 1)
    sizes = sizes.at[1:1 + 2 * couples:2].set(source_of - shifted).at[2:2 + 2 * couples:2].set(receiver + shifted)
    return sizes[jax.random.permutation(jax.random.fold_in(rng, 2), amount)]


def noise(key, shape, scale, reach, cuts=(), kind=jnp.bfloat16):
    drawn = scale * jax.random.normal(key, shape, jnp.float32)
    if cuts:
        drawn = drawn * level_of(key, shape, cuts, -0.22, 0.18)
    return jnp.clip(drawn, -reach, reach).astype(kind)


def setup_inputs(seed: int = 0) -> dict:
    key_list = jax.random.split(jax.random.key(seed), 40)
    return {
        "entering_activations": noise(key_list[0], (TOKENS, D), 1.0, 6.0, ((0, 32),), jnp.float32),
        "segment_ids": jax.vmap(lambda own: jnp.searchsorted(jnp.cumsum(ragged(own, DOCS, SEQ_LEN, SEQ_LEN // 2, 2)), jnp.arange(SEQ_LEN), side="right"))(jax.random.split(key_list[1], SEQS)).reshape((SEQS, SEQ_LEN)).astype(jnp.int32),
        "leaving_activation_slope": noise(key_list[2], (TOKENS, D), 1.0, 6.0, ((0, 32),), jnp.float32),
        "qkv_weight": noise(key_list[3], (D, 3 * D), D ** -0.5, 0.1875, ((0, 16), (1, 2)), jnp.float32),
        "qv_bias": noise(key_list[4], (2 * D,), 0.3, 1.75, ((0, 2),), jnp.float32),
        "dense_weight": noise(key_list[5], (D, D), (D // 8) ** -0.5, 0.5, ((0, 2), (1, 16)), jnp.float32),
        "dense_bias": noise(key_list[6], (D,), 0.3, 1.75, (), jnp.float32),
        "up_weight": noise(key_list[7], (D, FF), D ** -0.5, 0.1875, ((0, 16), (1, 2)), jnp.float32),
        "up_bias": noise(key_list[8], (FF,), 0.5, 3.0, ((0, 2),), jnp.float32),
        "down_weight": noise(key_list[9], (FF, D), FF ** -0.5, 0.09375, ((0, 2), (1, 16)), jnp.float32),
        "down_bias": noise(key_list[10], (D,), 0.3, 1.75, (), jnp.float32),
        "mixer_scale_factor": jnp.clip(1.0 + 0.18 * jax.random.normal(key_list[11], (D,), jnp.float32), 0.1, 1.9),
        "mixer_offset_term": noise(key_list[12], (D,), 0.3, 1.75, (), jnp.float32),
        "perceptron_scale_factor": jnp.clip(1.0 + 0.18 * jax.random.normal(key_list[13], (D,), jnp.float32), 0.1, 1.9),
        "perceptron_offset_term": noise(key_list[14], (D,), 0.3, 1.75, (), jnp.float32),
        "first_qkv_weight": noise(key_list[15], (D, 3 * D), 4.0, 24.0, ((0, 16), (1, 2)), jnp.float32),
        "first_qv_bias": noise(key_list[16], (2 * D,), 4.0, 24.0, ((0, 2),), jnp.float32),
        "first_dense_weight": noise(key_list[17], (D, D), 4.0, 24.0, ((0, 2), (1, 16)), jnp.float32),
        "first_dense_bias": noise(key_list[18], (D,), 10.0, 64.0, (), jnp.float32),
        "first_up_weight": noise(key_list[19], (D, FF), 4.0, 24.0, ((0, 16), (1, 2)), jnp.float32),
        "first_up_bias": noise(key_list[20], (FF,), 4.0, 24.0, ((0, 2),), jnp.float32),
        "first_down_weight": noise(key_list[21], (FF, D), 4.0, 24.0, ((0, 2), (1, 16)), jnp.float32),
        "first_down_bias": noise(key_list[22], (D,), 10.0, 64.0, (), jnp.float32),
        "first_norm1_gain": noise(key_list[23], (D,), 10.0, 64.0, (), jnp.float32),
        "first_norm1_bias": noise(key_list[24], (D,), 10.0, 64.0, (), jnp.float32),
        "first_norm2_gain": noise(key_list[25], (D,), 10.0, 64.0, (), jnp.float32),
        "first_norm2_bias": noise(key_list[26], (D,), 10.0, 64.0, (), jnp.float32),
        "second_qkv_weight": jnp.clip(jnp.exp(math.log(2048.0) - 3.465736 * jax.random.uniform(key_list[27], (D, 3 * D), jnp.float32) ** level_of(key_list[27], (D, 3 * D), ((0, 16), (1, 2)), -0.2, 0.2)), 64.0, 2048.0),
        "second_qv_bias": jnp.clip(jnp.exp(math.log(2048.0) - 3.465736 * jax.random.uniform(key_list[28], (2 * D,), jnp.float32) ** level_of(key_list[28], (2 * D,), ((0, 2),), -0.2, 0.2)), 64.0, 2048.0),
        "second_dense_weight": jnp.clip(jnp.exp(math.log(2048.0) - 3.465736 * jax.random.uniform(key_list[29], (D, D), jnp.float32) ** level_of(key_list[29], (D, D), ((0, 2), (1, 16)), -0.2, 0.2)), 64.0, 2048.0),
        "second_dense_bias": jnp.clip(jnp.exp(jax.random.uniform(key_list[30], (D,), jnp.float32, math.log(1024.0), math.log(16384.0))), 1024.0, 16384.0),
        "second_up_weight": jnp.clip(jnp.exp(math.log(2048.0) - 3.465736 * jax.random.uniform(key_list[31], (D, FF), jnp.float32) ** level_of(key_list[31], (D, FF), ((0, 16), (1, 2)), -0.2, 0.2)), 64.0, 2048.0),
        "second_up_bias": jnp.clip(jnp.exp(math.log(2048.0) - 3.465736 * jax.random.uniform(key_list[32], (FF,), jnp.float32) ** level_of(key_list[32], (FF,), ((0, 2),), -0.2, 0.2)), 64.0, 2048.0),
        "second_down_weight": jnp.clip(jnp.exp(math.log(2048.0) - 3.465736 * jax.random.uniform(key_list[33], (FF, D), jnp.float32) ** level_of(key_list[33], (FF, D), ((0, 2), (1, 16)), -0.2, 0.2)), 64.0, 2048.0),
        "second_down_bias": jnp.clip(jnp.exp(jax.random.uniform(key_list[34], (D,), jnp.float32, math.log(1024.0), math.log(16384.0))), 1024.0, 16384.0),
        "second_norm1_gain": jnp.clip(jnp.exp(jax.random.uniform(key_list[35], (D,), jnp.float32, math.log(1024.0), math.log(16384.0))), 1024.0, 16384.0),
        "second_norm1_bias": jnp.clip(jnp.exp(jax.random.uniform(key_list[36], (D,), jnp.float32, math.log(1024.0), math.log(16384.0))), 1024.0, 16384.0),
        "second_norm2_gain": jnp.clip(jnp.exp(jax.random.uniform(key_list[37], (D,), jnp.float32, math.log(1024.0), math.log(16384.0))), 1024.0, 16384.0),
        "second_norm2_bias": jnp.clip(jnp.exp(jax.random.uniform(key_list[38], (D,), jnp.float32, math.log(1024.0), math.log(16384.0))), 1024.0, 16384.0),
    }


beta_first = 0.9
beta_second = 0.95

def rounded(values):
    return lax.optimization_barrier(values.astype(jnp.bfloat16)).astype(jnp.float32)

def standardise_features(values, elementwise_multiplier, additive_offset):
    feature_midpoint = lax.optimization_barrier(jnp.mean(values, axis=-1, keepdims=True))
    demeaned_entries = values - feature_midpoint
    reciprocal_spread = lax.rsqrt(lax.optimization_barrier(jnp.mean(demeaned_entries * demeaned_entries, axis=-1, keepdims=True)) + 1e-05)
    unit_spread_entries = demeaned_entries * reciprocal_spread
    return ((unit_spread_entries * elementwise_multiplier + additive_offset).astype(jnp.bfloat16), unit_spread_entries, reciprocal_spread)

def standardise_features_reverse(loss_slope, unit_spread_entries, reciprocal_spread, elementwise_multiplier):
    multiplied_entries = loss_slope * elementwise_multiplier
    return reciprocal_spread * (multiplied_entries - lax.optimization_barrier(jnp.mean(multiplied_entries, axis=-1, keepdims=True)) - unit_spread_entries * lax.optimization_barrier(jnp.mean(multiplied_entries * unit_spread_entries, axis=-1, keepdims=True)))

def gelu_parts(pre):
    inner = 0.7978845608 * (pre + 0.044715 * pre * pre * pre)
    tanh_val = jnp.tanh(inner)
    value = 0.5 * pre * (1.0 + tanh_val)
    slope = 0.5 * (1.0 + tanh_val) + 0.5 * pre * (1.0 - tanh_val * tanh_val) * 0.7978845608 * (1.0 + 3.0 * 0.044715 * pre * pre)
    return (value, slope)

def grouped(left, right):
    rows, inner = left.shape
    width = inner // N_TENSOR
    parts = jnp.einsum('lgc,gcn->gln', left.reshape(rows, N_TENSOR, width).astype(jnp.float32), right.reshape(N_TENSOR, width, right.shape[1]).astype(jnp.float32))
    return lax.optimization_barrier(jnp.sum(rounded(parts), axis=0))

def head_slopes(first, count):
    index = (first + jnp.arange(count)).astype(jnp.float32)
    return jnp.exp2(-8.0 * (index + 1.0) / FOCUS_COUNT)

def full_bias(qv_bias, heads):
    pair = qv_bias.reshape(heads, 2, HEAD_DIM)
    return jnp.stack([pair[:, 0], jnp.zeros_like(pair[:, 0]), pair[:, 1]], axis=1).reshape(heads * 3 * HEAD_DIM)

def masked_scores(query, keys, start, segments, slopes):
    block = query.shape[0]
    length = keys.shape[0]
    raw = jnp.einsum('qhd,khd->hqk', query, keys) * HEAD_DIM ** (-0.5)
    rows = start + jnp.arange(block)
    cols = jnp.arange(length)
    offset = (cols[None, :] - rows[:, None]).astype(jnp.float32)
    seg_rows = segments[start:start + block]
    allowed = (cols[None, :] <= rows[:, None]) & (seg_rows[:, None] == segments[None, :])
    return jnp.where(allowed[None], raw + slopes[:, None, None] * offset[None], -1e+30)

def split_heads(qkv_low):
    length = qkv_low.shape[0]
    heads = qkv_low.shape[1] // (3 * HEAD_DIM)
    split = qkv_low.reshape(length, heads, 3, HEAD_DIM).astype(jnp.float32)
    return (split[:, :, 0], split[:, :, 1], split[:, :, 2], heads)

def attention_forward(qkv_low, segments, slopes):
    query, keys, values, heads = split_heads(qkv_low)
    length = query.shape[0]
    block = min(512, length)
    contexts = []
    totals = []
    for start in range(0, length, block):
        scores = masked_scores(query[start:start + block], keys, start, segments, slopes)
        peak = lax.optimization_barrier(jnp.max(scores, axis=-1, keepdims=True))
        total = peak + jnp.log(lax.optimization_barrier(jnp.sum(jnp.exp(scores - peak), axis=-1, keepdims=True)))
        probs = rounded(jnp.exp(scores - total))
        context = jnp.einsum('hqk,khd->qhd', probs, values)
        contexts.append(context.reshape(block, heads * HEAD_DIM).astype(jnp.bfloat16))
        totals.append(total)
    return (jnp.concatenate(contexts, axis=0), totals)

def attention_backward(qkv_low, segments, slopes, totals, dcontext):
    query, keys, values, heads = split_heads(qkv_low)
    length = query.shape[0]
    block = min(512, length)
    scale = HEAD_DIM ** (-0.5)
    dkeys = jnp.zeros(keys.shape, jnp.float32)
    dvalues = jnp.zeros(values.shape, jnp.float32)
    dquery_parts = []
    for number, start in enumerate(range(0, length, block)):
        scores = masked_scores(query[start:start + block], keys, start, segments, slopes)
        probs = jnp.exp(scores - totals[number])
        probs_low = rounded(probs)
        grad_block = dcontext[start:start + block].reshape(block, heads, HEAD_DIM).astype(jnp.float32)
        dvalues = dvalues + jnp.einsum('hqk,qhd->khd', probs_low, grad_block)
        dprob = jnp.einsum('qhd,khd->hqk', grad_block, values)
        delta = lax.optimization_barrier(jnp.sum(probs * dprob, axis=-1, keepdims=True))
        dscore = rounded(probs * (dprob - delta))
        dquery_parts.append(jnp.einsum('hqk,khd->qhd', dscore, keys) * scale)
        dkeys = dkeys + jnp.einsum('hqk,qhd->khd', dscore, query[start:start + block]) * scale
    dquery = jnp.concatenate(dquery_parts, axis=0)
    return jnp.stack([dquery, dkeys, dvalues], axis=2).reshape(length, heads * 3 * HEAD_DIM)

def query_value_slope(packed_triple_sensitivity, heads):
    split = packed_triple_sensitivity.reshape(packed_triple_sensitivity.shape[0], heads, 3, HEAD_DIM)
    pair = jnp.stack([split[:, :, 0], split[:, :, 2]], axis=2)
    return lax.optimization_barrier(jnp.sum(pair, axis=0)).reshape(heads * 2 * HEAD_DIM)

def sequence_pass(local_token_activations, seg_seq, local_tokens_sensitivity, lows, vectors):
    qkv_low, dense_low, up_low, down_low = lows
    qv_bias, dense_bias, up_bias, down_bias, mixer_multiplier, mixer_additive_offset, perceptron_multiplier, perceptron_additive_offset = vectors
    slopes = head_slopes(0, FOCUS_COUNT)
    mixer_standardised, mixer_unit_spread1, mixer_reciprocal_spread1 = standardise_features(local_token_activations, mixer_multiplier, mixer_additive_offset)
    qkv = (jnp.dot(mixer_standardised, qkv_low, preferred_element_type=jnp.float32) + full_bias(qv_bias, FOCUS_COUNT)).astype(jnp.bfloat16)
    context, totals = attention_forward(qkv, seg_seq, slopes)
    skip_path_sum = local_token_activations + grouped(context, dense_low) + dense_bias
    perceptron_standardised, perceptron_unit_spread2, perceptron_reciprocal_spread2 = standardise_features(skip_path_sum, perceptron_multiplier, perceptron_additive_offset)
    pre = jnp.dot(perceptron_standardised, up_low, preferred_element_type=jnp.float32) + up_bias
    act_val, act_slope = gelu_parts(pre)
    act = act_val.astype(jnp.bfloat16)
    block_out = skip_path_sum + grouped(act, down_low) + down_bias
    out_low = local_tokens_sensitivity.astype(jnp.bfloat16)
    contraction_sensitivity = jnp.dot(act.T, out_low, preferred_element_type=jnp.float32)
    hidden_activation_sensitivity = jnp.dot(out_low, down_low.T, preferred_element_type=jnp.float32) * act_slope
    dpre_low = hidden_activation_sensitivity.astype(jnp.bfloat16)
    expansion_sensitivity = jnp.dot(perceptron_standardised.T, dpre_low, preferred_element_type=jnp.float32)
    pre_perceptron_sensitivity = grouped(dpre_low, up_low.T)
    skip_path_sensitivity = local_tokens_sensitivity + standardise_features_reverse(pre_perceptron_sensitivity, perceptron_unit_spread2, perceptron_reciprocal_spread2, perceptron_multiplier)
    dresid_low = skip_path_sensitivity.astype(jnp.bfloat16)
    mixer_merge_sensitivity = jnp.dot(context.T, dresid_low, preferred_element_type=jnp.float32)
    dcontext = jnp.dot(dresid_low, dense_low.T, preferred_element_type=jnp.float32).astype(jnp.bfloat16)
    packed_triple_sensitivity = attention_backward(qkv, seg_seq, slopes, totals, dcontext)
    dqkv_low = packed_triple_sensitivity.astype(jnp.bfloat16)
    packed_triple_slope = jnp.dot(mixer_standardised.T, dqkv_low, preferred_element_type=jnp.float32)
    pre_mixer_sensitivity = grouped(dqkv_low, qkv_low.T)
    entering_sensitivity = skip_path_sensitivity + standardise_features_reverse(pre_mixer_sensitivity, mixer_unit_spread1, mixer_reciprocal_spread1, mixer_multiplier)
    parameter_slopes = (packed_triple_slope, query_value_slope(packed_triple_sensitivity, FOCUS_COUNT), mixer_merge_sensitivity, lax.optimization_barrier(jnp.sum(skip_path_sensitivity, axis=0)), expansion_sensitivity, lax.optimization_barrier(jnp.sum(hidden_activation_sensitivity, axis=0)), contraction_sensitivity, lax.optimization_barrier(jnp.sum(local_tokens_sensitivity, axis=0)), lax.optimization_barrier(jnp.sum(pre_mixer_sensitivity * mixer_unit_spread1, axis=0)), lax.optimization_barrier(jnp.sum(pre_mixer_sensitivity, axis=0)), lax.optimization_barrier(jnp.sum(pre_perceptron_sensitivity * perceptron_unit_spread2, axis=0)), lax.optimization_barrier(jnp.sum(pre_perceptron_sensitivity, axis=0)))
    return (block_out, entering_sensitivity, parameter_slopes)

def adamw(param, loss_slope, first, second, rate, decay):
    first_new = beta_first * first + (1.0 - beta_first) * loss_slope
    second_new = beta_second * second + (1.0 - beta_second) * loss_slope * loss_slope
    update = first_new / (1.0 - beta_first ** ADAM_STEP) / (jnp.sqrt(second_new / (1.0 - beta_second ** ADAM_STEP)) + 1e-08)
    return (param - rate * (update + decay * param), first_new, second_new)

def reference(entering_activations, segment_ids, leaving_activation_slope, qkv_weight, qv_bias, dense_weight, dense_bias, up_weight, up_bias, down_weight, down_bias, mixer_scale_factor, mixer_offset_term, perceptron_scale_factor, perceptron_offset_term, first_qkv_weight, first_qv_bias, first_dense_weight, first_dense_bias, first_up_weight, first_up_bias, first_down_weight, first_down_bias, first_norm1_gain, first_norm1_bias, first_norm2_gain, first_norm2_bias, second_qkv_weight, second_qv_bias, second_dense_weight, second_dense_bias, second_up_weight, second_up_bias, second_down_weight, second_down_bias, second_norm1_gain, second_norm1_bias, second_norm2_gain, second_norm2_bias):
    params = (qkv_weight, qv_bias, dense_weight, dense_bias, up_weight, up_bias, down_weight, down_bias, mixer_scale_factor, mixer_offset_term, perceptron_scale_factor, perceptron_offset_term)
    firsts = (first_qkv_weight, first_qv_bias, first_dense_weight, first_dense_bias, first_up_weight, first_up_bias, first_down_weight, first_down_bias, first_norm1_gain, first_norm1_bias, first_norm2_gain, first_norm2_bias)
    seconds = (second_qkv_weight, second_qv_bias, second_dense_weight, second_dense_bias, second_up_weight, second_up_bias, second_down_weight, second_down_bias, second_norm1_gain, second_norm1_bias, second_norm2_gain, second_norm2_bias)
    lows = (qkv_weight.astype(jnp.bfloat16), dense_weight.astype(jnp.bfloat16), up_weight.astype(jnp.bfloat16), down_weight.astype(jnp.bfloat16))
    vectors = (qv_bias, dense_bias, up_bias, down_bias, mixer_scale_factor, mixer_offset_term, perceptron_scale_factor, perceptron_offset_term)
    inputs = entering_activations.reshape(SEQS, SEQ_LEN, D)
    cotangents = leaving_activation_slope.reshape(SEQS, SEQ_LEN, D)

    def one_sequence(carry, item):
        local_token_activations, seg_seq, local_tokens_sensitivity = item
        block_out, entering_sensitivity, parameter_slopes = sequence_pass(local_token_activations, seg_seq, local_tokens_sensitivity, lows, vectors)
        return (tuple((total + part for total, part in zip(carry, parameter_slopes))), (block_out, entering_sensitivity))
    start = tuple((jnp.zeros(p.shape, jnp.float32) for p in params))
    sums, (outs, grad_ins) = lax.scan(one_sequence, start, (inputs, segment_ids, cotangents))
    results = []
    for index in range(12):
        matrix = index in (0, 2, 4, 6)
        results.append(adamw(params[index], sums[index], firsts[index], seconds[index], 0.01 if matrix else 0.1, 0.1 if matrix else 0.0))
    news = [r[0] for r in results]
    moments_one = [r[1] for r in results]
    moments_two = [r[2] for r in results]
    return (outs.reshape(TOKENS, D), grad_ins.reshape(TOKENS, D), *sums, *news, *moments_one, *moments_two)
```

```python
import functools

import jax
import jax.numpy as jnp
from jax import lax
from jax.experimental import pallas as pl
from jax.experimental.pallas import tpu as pltpu
from jax.sharding import PartitionSpec as P

D = 1024
FOCUS_COUNT = 16
FF = 4096
ADAM_STEP = 4
HEAD_DIM = 64
MAX_SPAN = 512


beta_first = 0.9
beta_second = 0.95


def standardise_features(values, elementwise_multiplier, additive_offset):
    feature_midpoint = jnp.mean(values, axis=-1, keepdims=True)
    demeaned_entries = values - feature_midpoint
    reciprocal_spread = lax.rsqrt(
        jnp.mean(demeaned_entries * demeaned_entries, axis=-1, keepdims=True) + 1e-05
    )
    unit_spread_entries = demeaned_entries * reciprocal_spread
    return (
        (unit_spread_entries * elementwise_multiplier + additive_offset).astype(jnp.bfloat16),
        unit_spread_entries,
        reciprocal_spread,
    )


def standardise_features_reverse(
    loss_slope, unit_spread_entries, reciprocal_spread, elementwise_multiplier
):
    multiplied_entries = loss_slope * elementwise_multiplier
    return reciprocal_spread * (
        multiplied_entries
        - jnp.mean(multiplied_entries, axis=-1, keepdims=True)
        - unit_spread_entries
        * jnp.mean(multiplied_entries * unit_spread_entries, axis=-1, keepdims=True)
    )


def gelu_parts(pre):
    inner = 0.7978845608 * (pre + 0.044715 * pre * pre * pre)
    tanh_val = jnp.tanh(inner)
    value = 0.5 * pre * (1.0 + tanh_val)
    slope = 0.5 * (1.0 + tanh_val) + 0.5 * pre * (1.0 - tanh_val * tanh_val) * 0.7978845608 * (
        1.0 + 3.0 * 0.044715 * pre * pre
    )
    return (value, slope)


def inner_rows(left, right):
    return lax.dot_general(
        left, right, (((0,), (0,)), ((), ())), preferred_element_type=jnp.float32
    )


def times_transposed(left, right):
    return lax.dot_general(
        left, right, (((1,), (1,)), ((), ())), preferred_element_type=jnp.float32
    )


def head_slopes(first, count):
    index = (first + jnp.arange(count)).astype(jnp.float32)
    return jnp.exp2(-8.0 * (index + 1.0) / FOCUS_COUNT)


def full_bias(qv_bias, heads):
    pair = qv_bias.reshape(heads, 2, HEAD_DIM)
    return jnp.stack([pair[:, 0], jnp.zeros_like(pair[:, 0]), pair[:, 1]], axis=1).reshape(
        heads * 3 * HEAD_DIM
    )


def window(start, block, length):
    return (max(0, start - MAX_SPAN), min(length, start + block))


def fill_offsets(offsets, rows_seg, cols_seg, rows_first, length, block):
    for start in range(0, length, block):
        low, high = window(start, block, length)
        shape = (block, high - low) if rows_first else (high - low, block)
        axis = 0 if rows_first else 1
        row = start + lax.broadcasted_iota(jnp.int32, shape, axis)
        col = low + lax.broadcasted_iota(jnp.int32, shape, 1 - axis)
        if rows_first:
            same = rows_seg[start : start + block, :] == cols_seg[:, low:high]
        else:
            same = rows_seg[low:high, :] == cols_seg[:, start : start + block]
        allowed = (col <= row) & same
        value = jnp.where(allowed, (col - row).astype(jnp.float32), -1e30)
        if rows_first:
            offsets[start : start + block, 0 : high - low] = value
        else:
            offsets[0 : high - low, start : start + block] = value


def forward_kernel(block, slopes, x, rows_seg, cols_seg, out, offsets):
    length = x.shape[0]
    step = pl.program_id(0)

    @pl.when(step == 0)
    def _():
        fill_offsets(offsets, rows_seg, cols_seg, True, length, block)

    for i in range(2):
        base = 3 * HEAD_DIM * i
        slope = slopes[2 * step + i]
        query = x[:, base : base + HEAD_DIM] * HEAD_DIM ** (-0.5)
        keys = x[:, base + HEAD_DIM : base + 2 * HEAD_DIM]
        values = x[:, base + 2 * HEAD_DIM : base + 3 * HEAD_DIM]
        for start in range(0, length, block):
            low, high = window(start, block, length)
            scores = (
                times_transposed(query[start : start + block], keys[low:high])
                + slope * offsets[start : start + block, 0 : high - low]
            )
            peak = jnp.max(scores, axis=1, keepdims=True)
            raised = jnp.exp(scores - peak)
            total = jnp.sum(raised, axis=1, keepdims=True)
            probs = (raised * (1.0 / total)).astype(jnp.bfloat16)
            context = jnp.dot(probs, values[low:high], preferred_element_type=jnp.float32)
            out[start : start + block, HEAD_DIM * i : HEAD_DIM * (i + 1)] = context.astype(
                jnp.bfloat16
            )


def backward_kernel(
    block, slopes, x, grad, rows_seg, cols_seg, out, sums, offsets, dkeys, dvalues, dquery
):
    length = x.shape[0]
    step = pl.program_id(0)
    scale = HEAD_DIM ** (-0.5)

    @pl.when(step == 0)
    def _():
        fill_offsets(offsets, rows_seg, cols_seg, False, length, block)

    for i in range(2):
        base = 3 * HEAD_DIM * i
        slope = slopes[2 * step + i]
        query = x[:, base : base + HEAD_DIM] * scale
        keys = x[:, base + HEAD_DIM : base + 2 * HEAD_DIM]
        values = x[:, base + 2 * HEAD_DIM : base + 3 * HEAD_DIM]
        slopes_out = grad[:, HEAD_DIM * i : HEAD_DIM * (i + 1)]
        dkeys[...] = jnp.zeros_like(dkeys)
        dvalues[...] = jnp.zeros_like(dvalues)
        for start in range(0, length, block):
            low, high = window(start, block, length)
            query_block = query[start : start + block]
            grad_block = slopes_out[start : start + block]
            scores = (
                times_transposed(keys[low:high], query_block)
                + slope * offsets[0 : high - low, start : start + block]
            )
            peak = jnp.max(scores, axis=0, keepdims=True)
            raised = jnp.exp(scores - peak)
            total = jnp.sum(raised, axis=0, keepdims=True)
            probs = raised * (1.0 / total)
            dprob = times_transposed(values[low:high], grad_block)
            delta = jnp.sum(probs * dprob, axis=0, keepdims=True)
            dscore = (probs * (dprob - delta)).astype(jnp.bfloat16)
            dvalues[low:high, :] += jnp.dot(
                probs.astype(jnp.bfloat16), grad_block, preferred_element_type=jnp.float32
            )
            dkeys[low:high, :] += jnp.dot(dscore, query_block, preferred_element_type=jnp.float32)
            dquery[start : start + block, :] = inner_rows(dscore, keys[low:high]) * scale
        for place, part in enumerate((dquery, dkeys, dvalues)):
            first = base + HEAD_DIM * place
            out[:, first : first + HEAD_DIM] = part[...].astype(jnp.bfloat16)
            sums[:, first : first + HEAD_DIM] = jnp.sum(part[...], axis=0, keepdims=True)


def attention_forward(qkv, segments, slopes):
    length, width = qkv.shape
    pairs = width // (6 * HEAD_DIM)
    block = min(256, length)
    span = min(length, block + MAX_SPAN)
    return pl.pallas_call(
        functools.partial(forward_kernel, block),
        grid=(pairs,),
        out_shape=jax.ShapeDtypeStruct((length, width // 3), jnp.bfloat16),
        in_specs=[
            pl.BlockSpec(memory_space=pltpu.SMEM),
            pl.BlockSpec((length, 6 * HEAD_DIM), lambda p: (0, p)),
            pl.BlockSpec((length, 1), lambda p: (0, 0)),
            pl.BlockSpec((1, length), lambda p: (0, 0)),
        ],
        out_specs=pl.BlockSpec((length, 2 * HEAD_DIM), lambda p: (0, p)),
        scratch_shapes=[pltpu.VMEM((length, span), jnp.float32)],
        cost_estimate=pl.CostEstimate(
            flops=4 * length * span * width // 3,
            bytes_accessed=8 * length * width // 3,
            transcendentals=length * span * pairs * 2,
        ),
        compiler_params=pltpu.CompilerParams(vmem_limit_bytes=40 * 1024 * 1024),
        name="attention_forward",
    )(slopes, qkv, segments[:, None], segments[None, :])


def attention_backward(qkv, segments, slopes, dcontext):
    length, width = qkv.shape
    pairs = width // (6 * HEAD_DIM)
    block = min(256, length)
    span = min(length, block + MAX_SPAN)
    return pl.pallas_call(
        functools.partial(backward_kernel, block),
        grid=(pairs,),
        out_shape=(
            jax.ShapeDtypeStruct((length, width), jnp.bfloat16),
            jax.ShapeDtypeStruct((1, width), jnp.float32),
        ),
        in_specs=[
            pl.BlockSpec(memory_space=pltpu.SMEM),
            pl.BlockSpec((length, 6 * HEAD_DIM), lambda p: (0, p)),
            pl.BlockSpec((length, 2 * HEAD_DIM), lambda p: (0, p)),
            pl.BlockSpec((length, 1), lambda p: (0, 0)),
            pl.BlockSpec((1, length), lambda p: (0, 0)),
        ],
        out_specs=(
            pl.BlockSpec((length, 6 * HEAD_DIM), lambda p: (0, p)),
            pl.BlockSpec((1, 6 * HEAD_DIM), lambda p: (0, p)),
        ),
        scratch_shapes=[
            pltpu.VMEM((span, length), jnp.float32),
            pltpu.VMEM((length, HEAD_DIM), jnp.float32),
            pltpu.VMEM((length, HEAD_DIM), jnp.float32),
            pltpu.VMEM((length, HEAD_DIM), jnp.float32),
        ],
        cost_estimate=pl.CostEstimate(
            flops=10 * length * span * width // 3,
            bytes_accessed=14 * length * width // 3,
            transcendentals=length * span * pairs * 2,
        ),
        compiler_params=pltpu.CompilerParams(vmem_limit_bytes=40 * 1024 * 1024),
        name="attention_backward",
    )(slopes, qkv, dcontext, segments[:, None], segments[None, :])


def swap(values):
    return lax.ppermute(values, "tensor", [(0, 1), (1, 0)])


def spread(values, count):
    if count == 2:
        return [values, swap(values)]
    return [lax.all_gather(values, "tensor", axis=0, tiled=True)]


def fold(parts, count):
    if count == 2:
        return swap(parts[1]).astype(jnp.float32) + parts[0].astype(jnp.float32)
    return lax.psum_scatter(parts[0], "tensor", scatter_dimension=0, tiled=True).astype(
        jnp.float32
    )


def to_order(parts, rank):
    if len(parts) == 2:
        own, other = parts
        return jnp.concatenate(
            [jnp.where(rank == 0, own, other), jnp.where(rank == 0, other, own)], axis=0
        )
    return parts[0]


def from_order(values, rank, count):
    if count == 2:
        half = values.shape[0] // 2
        return [
            lax.dynamic_slice_in_dim(values, rank * half, half, 0),
            lax.dynamic_slice_in_dim(values, (1 - rank) * half, half, 0),
        ]
    return [values]


def product(left, right):
    return jnp.dot(left, right, preferred_element_type=jnp.float32)


def add_up(lefts, rights):
    total = inner_rows(lefts[0], rights[0])
    for left, right in zip(lefts[1:], rights[1:]):
        total = total + inner_rows(left, right)
    return total


def total_over_all(vector, shared, rank):
    rows = lax.all_gather(vector[None], ("dp", "tensor"), axis=0, tiled=True)
    everyone = jnp.sum(rows[:, :shared], axis=0)
    count = lax.axis_size("tensor")
    split = rows[:, shared:].reshape(rows.shape[0] // count, count, -1)
    mine = lax.dynamic_index_in_dim(jnp.sum(split, axis=0), rank, 0, keepdims=False)
    return everyone, mine


def adamw(param, loss_slope, first, second, rate, decay):
    first_new = beta_first * first + (1.0 - beta_first) * loss_slope
    second_new = beta_second * second + (1.0 - beta_second) * loss_slope * loss_slope
    update = (
        first_new
        / (1.0 - beta_first**ADAM_STEP)
        / (jnp.sqrt(second_new / (1.0 - beta_second**ADAM_STEP)) + 1e-08)
    )
    return (param - rate * (update + decay * param), first_new, second_new)


def local(
    entering_activations,
    segment_ids,
    leaving_activation_slope,
    qkv_weight,
    qv_bias,
    dense_weight,
    dense_bias,
    up_weight,
    up_bias,
    down_weight,
    down_bias,
    mixer_scale_factor,
    mixer_offset_term,
    perceptron_scale_factor,
    perceptron_offset_term,
    first_qkv_weight,
    first_qv_bias,
    first_dense_weight,
    first_dense_bias,
    first_up_weight,
    first_up_bias,
    first_down_weight,
    first_down_bias,
    first_norm1_gain,
    first_norm1_bias,
    first_norm2_gain,
    first_norm2_bias,
    second_qkv_weight,
    second_qv_bias,
    second_dense_weight,
    second_dense_bias,
    second_up_weight,
    second_up_bias,
    second_down_weight,
    second_down_bias,
    second_norm1_gain,
    second_norm1_bias,
    second_norm2_gain,
    second_norm2_bias,
):
    params = (
        qkv_weight,
        qv_bias,
        dense_weight,
        dense_bias,
        up_weight,
        up_bias,
        down_weight,
        down_bias,
        mixer_scale_factor,
        mixer_offset_term,
        perceptron_scale_factor,
        perceptron_offset_term,
    )
    firsts = (
        first_qkv_weight,
        first_qv_bias,
        first_dense_weight,
        first_dense_bias,
        first_up_weight,
        first_up_bias,
        first_down_weight,
        first_down_bias,
        first_norm1_gain,
        first_norm1_bias,
        first_norm2_gain,
        first_norm2_bias,
    )
    seconds = (
        second_qkv_weight,
        second_qv_bias,
        second_dense_weight,
        second_dense_bias,
        second_up_weight,
        second_up_bias,
        second_down_weight,
        second_down_bias,
        second_norm1_gain,
        second_norm1_bias,
        second_norm2_gain,
        second_norm2_bias,
    )
    qkv_low, dense_low, up_low, down_low = (
        lax.all_gather(qkv_weight.astype(jnp.bfloat16), "dp", axis=0, tiled=True),
        lax.all_gather(dense_weight.astype(jnp.bfloat16), "dp", axis=1, tiled=True),
        lax.all_gather(up_weight.astype(jnp.bfloat16), "dp", axis=0, tiled=True),
        lax.all_gather(down_weight.astype(jnp.bfloat16), "dp", axis=1, tiled=True),
    )
    local_heads = qkv_low.shape[1] // (3 * HEAD_DIM)
    tensor_rank = lax.axis_index("tensor")
    count = lax.axis_size("tensor")
    slopes = head_slopes(tensor_rank * local_heads, local_heads)
    segments = segment_ids[0]
    mixer_standardised, mixer_unit_spread1, mixer_reciprocal_spread1 = standardise_features(
        entering_activations, mixer_scale_factor, mixer_offset_term
    )
    ones = spread(mixer_standardised, count)
    outs = spread(leaving_activation_slope.astype(jnp.bfloat16), count)
    qkv_bias = full_bias(qv_bias, local_heads)
    qkv = to_order([(product(one, qkv_low) + qkv_bias).astype(jnp.bfloat16) for one in ones], tensor_rank)
    context = attention_forward(qkv, segments, slopes)
    contexts = from_order(context, tensor_rank, count)
    skip_path_sum = (
        entering_activations
        + fold([product(part, dense_low).astype(jnp.bfloat16) for part in contexts], count)
        + dense_bias
    )
    perceptron_standardised, perceptron_unit_spread2, perceptron_reciprocal_spread2 = (
        standardise_features(skip_path_sum, perceptron_scale_factor, perceptron_offset_term)
    )
    twos = spread(perceptron_standardised, count)
    acts, dpres, dpre_lows, pre_parts = [], [], [], []
    for two, out in zip(twos, outs):
        act_val, act_slope = gelu_parts(product(two, up_low) + up_bias)
        acts.append(act_val.astype(jnp.bfloat16))
        dpres.append(times_transposed(out, down_low) * act_slope)
        dpre_lows.append(dpres[-1].astype(jnp.bfloat16))
        pre_parts.append(times_transposed(dpre_lows[-1], up_low).astype(jnp.bfloat16))
    pre_perceptron_sensitivity = fold(pre_parts, count)
    block_out = (
        skip_path_sum
        + fold([product(act, down_low).astype(jnp.bfloat16) for act in acts], count)
        + down_bias
    )
    contraction_sensitivity = add_up(acts, outs).astype(jnp.bfloat16)
    expansion_sensitivity = add_up(twos, dpre_lows).astype(jnp.bfloat16)
    up_bias_part = sum(jnp.sum(dpre, axis=0) for dpre in dpres)
    skip_path_sensitivity = leaving_activation_slope + standardise_features_reverse(
        pre_perceptron_sensitivity,
        perceptron_unit_spread2,
        perceptron_reciprocal_spread2,
        perceptron_scale_factor,
    )
    resids = spread(skip_path_sensitivity.astype(jnp.bfloat16), count)
    mixer_merge_sensitivity = add_up(contexts, resids).astype(jnp.bfloat16)
    dcontext = to_order(
        [times_transposed(resid, dense_low).astype(jnp.bfloat16) for resid in resids], tensor_rank
    )
    dqkv_low, dqkv_sums = attention_backward(qkv, segments, slopes, dcontext)
    dqkv_lows = from_order(dqkv_low, tensor_rank, count)
    packed_triple_slope = add_up(ones, dqkv_lows).astype(jnp.bfloat16)
    triple = dqkv_sums.reshape(local_heads, 3, HEAD_DIM)
    qv_part = jnp.stack([triple[:, 0], triple[:, 2]], axis=1).reshape(-1)
    pre_mixer_sensitivity = fold(
        [times_transposed(part, qkv_low).astype(jnp.bfloat16) for part in dqkv_lows], count
    )
    entering_activation_slope = skip_path_sensitivity + standardise_features_reverse(
        pre_mixer_sensitivity, mixer_unit_spread1, mixer_reciprocal_spread1, mixer_scale_factor
    )
    early, up_bias_grad = total_over_all(
        jnp.concatenate(
            [
                jnp.sum(skip_path_sensitivity, axis=0),
                jnp.sum(leaving_activation_slope, axis=0),
                jnp.sum(pre_perceptron_sensitivity * perceptron_unit_spread2, axis=0),
                jnp.sum(pre_perceptron_sensitivity, axis=0),
                up_bias_part,
            ]
        ),
        4 * D,
        tensor_rank,
    )
    dense_bias_grad, down_bias_grad, gain_two_grad, shift_two_grad = jnp.split(early, 4)
    late, qv_bias_grad = total_over_all(
        jnp.concatenate(
            [
                jnp.sum(pre_mixer_sensitivity * mixer_unit_spread1, axis=0),
                jnp.sum(pre_mixer_sensitivity, axis=0),
                qv_part,
            ]
        ),
        2 * D,
        tensor_rank,
    )
    gain_one_grad, shift_one_grad = jnp.split(late, 2)
    packed_triple_slope, mixer_merge_sensitivity, expansion_sensitivity, contraction_sensitivity = (
        part.astype(jnp.float32)
        for part in (
            lax.psum_scatter(packed_triple_slope, "dp", scatter_dimension=0, tiled=True),
            lax.psum_scatter(mixer_merge_sensitivity, "dp", scatter_dimension=1, tiled=True),
            lax.psum_scatter(expansion_sensitivity, "dp", scatter_dimension=0, tiled=True),
            lax.psum_scatter(contraction_sensitivity, "dp", scatter_dimension=1, tiled=True),
        )
    )
    parameter_slopes = (
        packed_triple_slope,
        qv_bias_grad,
        mixer_merge_sensitivity,
        dense_bias_grad,
        expansion_sensitivity,
        up_bias_grad,
        contraction_sensitivity,
        down_bias_grad,
        gain_one_grad,
        shift_one_grad,
        gain_two_grad,
        shift_two_grad,
    )
    results = []
    for index in range(12):
        matrix = index in (0, 2, 4, 6)
        results.append(
            adamw(
                params[index],
                parameter_slopes[index],
                firsts[index],
                seconds[index],
                0.01 if matrix else 0.1,
                0.1 if matrix else 0.0,
            )
        )
    news = [r[0] for r in results]
    moments_one = [r[1] for r in results]
    moments_two = [r[2] for r in results]
    return (
        block_out,
        entering_activation_slope,
        *parameter_slopes,
        *news,
        *moments_one,
        *moments_two,
    )


def solution(mesh):
    in_specs = (
        P(("dp", "tensor"), None),
        P("dp", None),
        P(("dp", "tensor"), None),
        P("dp", "tensor"),
        P("tensor"),
        P("tensor", "dp"),
        P(),
        P("dp", "tensor"),
        P("tensor"),
        P("tensor", "dp"),
        P(),
        P(),
        P(),
        P(),
        P(),
        P("dp", "tensor"),
        P("tensor"),
        P("tensor", "dp"),
        P(),
        P("dp", "tensor"),
        P("tensor"),
        P("tensor", "dp"),
        P(),
        P(),
        P(),
        P(),
        P(),
        P("dp", "tensor"),
        P("tensor"),
        P("tensor", "dp"),
        P(),
        P("dp", "tensor"),
        P("tensor"),
        P("tensor", "dp"),
        P(),
        P(),
        P(),
        P(),
        P(),
    )
    out_specs = (
        P(("dp", "tensor"), None),
        P(("dp", "tensor"), None),
        P("dp", "tensor"),
        P("tensor"),
        P("tensor", "dp"),
        P(),
        P("dp", "tensor"),
        P("tensor"),
        P("tensor", "dp"),
        P(),
        P(),
        P(),
        P(),
        P(),
        P("dp", "tensor"),
        P("tensor"),
        P("tensor", "dp"),
        P(),
        P("dp", "tensor"),
        P("tensor"),
        P("tensor", "dp"),
        P(),
        P(),
        P(),
        P(),
        P(),
        P("dp", "tensor"),
        P("tensor"),
        P("tensor", "dp"),
        P(),
        P("dp", "tensor"),
        P("tensor"),
        P("tensor", "dp"),
        P(),
        P(),
        P(),
        P(),
        P(),
        P("dp", "tensor"),
        P("tensor"),
        P("tensor", "dp"),
        P(),
        P("dp", "tensor"),
        P("tensor"),
        P("tensor", "dp"),
        P(),
        P(),
        P(),
        P(),
        P(),
    )
    return jax.shard_map(local, mesh=mesh, in_specs=in_specs, out_specs=out_specs, check_vma=False)
```
